32 devices in a mesh: scene: 2 (over x), pulse: 16 (over z, y, core).
Axes of the slice: x: 2, y: 2, z: 4, core: 2. Of those that a mesh axis runs over, the one named last changes fastest.
Arguments:
- beams: bfloat16 [2, 2048, 4096], P(None, ('scene', 'pulse')), parts along dimension 1, may hold values from -6 to 6
- ukern: bfloat16 [2, 32], replicated, may hold values from -1 to 1
- rkern: float32 [16, 4], replicated, may hold values from -3 to 3
- angles: float32 [4, 2, 128], replicated, may hold values from -3.140625 to 3.140625
- taps: int32 [4, 2048], P(None, ('scene', 'pulse')), parts along dimension 1, may hold values from 0 to 15
- shifts: int32 [4, 16], replicated, may hold values from -48 to 48
- half_table: int32 [4, 16], replicated, may hold values from 0 to 1, as said below
Outputs:
- merged: bfloat16 [2, 2048, 4096], P(None, ('scene', 'pulse')), parts along dimension 1
The draws below stay inside these ranges and needn't reach their ends.
There are 2 independent parts, one for each index of `scene`. The reference program is written for one: setup_inputs(seed, part) draws one part's arguments, and reference() takes and returns one part's arrays. A program takes and returns all parts, laid end to end along the dimension named above; an argument that names none is the same for every part. Nothing has to cross between parts.
Inputs may be any that keep to these rules, and one draw needn't show every extreme that they name: half_table[l, s] + half_table[l, s XOR 2**l] == 1 for every level l and block s.
All inputs are finite; a program needn't handle non-finite values.
Results may differ from the reference program's by a relative error of at most 0.0074.
Values may be sent and summed in bfloat16 or wider, within the bound.
A program may use at most 64 MiB of HBM per device.

```python
import jax
import jax.numpy as jnp
from jax import lax

R = 4096
BEAMS = 64
UTAPS = 32
RTAPS = 4
PHASES = 16
SHIFT = 48
LEVELS = 4
NSUB = 16
ALLBEAMS = 1024


def draw_half_table(key, part):
    coins = jax.random.randint(jax.random.fold_in(key, 7), (LEVELS, NSUB), 0, 2).astype(jnp.int32)
    index = jnp.arange(NSUB, dtype=jnp.int32)
    rows = []
    for level in range(LEVELS):
        lower = jnp.bitwise_and(index, jnp.int32(NSUB - 1 - (1 << level)))
        bit = jnp.bitwise_and(jnp.right_shift(index, level), 1)
        rows.append(jnp.bitwise_xor(coins[level][lower], bit))
    return jnp.stack(rows).astype(jnp.int32)


def set_ends(array, key, least, largest):
    longest = array.shape.index(max(array.shape))
    spots = []
    for shift in (0, 1):
        where = [jax.random.randint(jax.random.fold_in(key, axis), (), 0, length) for axis, length in enumerate(array.shape)]
        where[longest] = (where[longest] + shift) % array.shape[longest]
        spots.append(tuple(where))
    return array.at[spots[0]].set(least).at[spots[1]].set(largest)


def shard_levels(stream_key, dims, shards, low, top_value):
    level, own = 1.0, jax.random.fold_in(stream_key, 6)
    for position, shards_of in shards:
        heights = jnp.exp(jax.random.uniform(jax.random.fold_in(own, position), (shards_of,), jnp.float32, low / len(shards), top_value / len(shards)))
        level = level * jnp.repeat(heights, dims[position] // shards_of).reshape([-1 if axis == position else 1 for axis in range(len(dims))])
    return level


def centred(key, extent, scale, reach, split=(), held_as=jnp.bfloat16):
    values = jax.random.normal(key, extent, jnp.float32) * scale
    if len(split) > 0:
        values = shard_levels(key, extent, split, -0.22, 0.18) * values
    return jnp.clip(values, min=-reach, max=reach).astype(held_as)


def setup_inputs(seed: int = 0, part: int = 0) -> dict:
    keys = jax.random.split(jax.random.key(seed), 8)
    part_splits = jax.random.split(jax.random.fold_in(keys[7], part), 8)
    return {
        "beams": centred(part_splits[0], (2, ALLBEAMS, R), 1.0, 6.0, ((1, 16),)),
        "ukern": centred(keys[1], (2, UTAPS), UTAPS ** -0.5, 1.0),
        "rkern": centred(keys[2], (PHASES, RTAPS), RTAPS ** -0.5, 3.0, (), jnp.float32),
        "angles": jnp.clip(jax.random.uniform(keys[3], (LEVELS, 2, 2 * BEAMS), jnp.float32, -3.140625, 3.140625), -3.140625, 3.140625),
        "taps": set_ends(jax.random.randint(part_splits[4], (LEVELS, ALLBEAMS), 0, PHASES), jax.random.fold_in(part_splits[4], 1), 0, PHASES - 1).astype(jnp.int32),
        "shifts": set_ends(jax.random.randint(keys[5], (LEVELS, NSUB), -SHIFT, SHIFT + 1), jax.random.fold_in(keys[5], 1), -SHIFT, SHIFT).astype(jnp.int32),
        "half_table": draw_half_table(jax.random.fold_in(keys[7], 71), part),
    }


def band_matrix(ukern, half, count, utaps):
    width = count // 2 + utaps
    local = jnp.arange(count, dtype=jnp.int32)
    rows = half * count + local
    cols = half * (count // 2) + jnp.arange(width, dtype=jnp.int32)
    offset = cols[None, :] - rows[:, None] // 2 - 1
    kernel = jnp.where((local % 2 == 0)[:, None], ukern[0].astype(jnp.float32)[None, :], ukern[1].astype(jnp.float32)[None, :])
    picks = (offset[:, :, None] == jnp.arange(utaps, dtype=jnp.int32)[None, None, :]).astype(jnp.float32)
    return jnp.sum(picks * kernel[:, None, :], axis=2)


def tap_weights(tap_row, rkern):
    onehot = (tap_row[:, None] == jnp.arange(rkern.shape[0], dtype=jnp.int32)[None, :]).astype(jnp.float32)
    return jnp.dot(onehot, rkern, precision=lax.Precision.HIGHEST, preferred_element_type=jnp.float32)


def child_term(range_band, sample_window, weights, shift, segment):
    blended_beam = jnp.einsum("dp,upe->ude", range_band, sample_window, precision=lax.Precision.HIGHEST, preferred_element_type=jnp.float32)
    length = blended_beam.shape[2]
    margin = SHIFT + RTAPS
    padded = jnp.pad(blended_beam, ((0, 0), (0, 0), (margin, margin)))
    shifted = jnp.zeros(blended_beam.shape, jnp.float32)
    for tap in range(RTAPS):
        piece = lax.dynamic_slice_in_dim(padded, margin + shift + tap - 1, length, 2)
        shifted = shifted + weights[None, :, tap, None] * piece
    cosine = jnp.cos(segment)[:, None]
    sine = jnp.sin(segment)[:, None]
    real_part = cosine * shifted[0] - sine * shifted[1]
    imag_part = sine * shifted[0] + cosine * shifted[1]
    return jnp.stack([real_part, imag_part])


def reference(beams, ukern, rkern, angles, taps, shifts, half_table):
    current = beams
    for level in range(LEVELS):
        def one_block(block_number):
            partner = jnp.bitwise_xor(block_number, 1 << level)
            half = half_table[level, block_number]
            range_band = band_matrix(ukern, half, BEAMS, UTAPS)
            weights = tap_weights(lax.dynamic_slice_in_dim(taps[level], block_number * BEAMS, BEAMS, 0), rkern)
            own_bit = jnp.bitwise_and(jnp.right_shift(block_number, level), 1)
            total = jnp.zeros((2, BEAMS, R), jnp.float32)
            for child, bit in ((block_number, own_bit), (partner, 1 - own_bit)):
                block = lax.dynamic_slice_in_dim(current, child * BEAMS, BEAMS, 1).astype(jnp.float32)
                padded = jnp.pad(block, ((0, 0), (UTAPS // 2, UTAPS // 2), (0, 0)))
                sample_window = lax.dynamic_slice_in_dim(padded, half * (BEAMS // 2), BEAMS // 2 + UTAPS, 1)
                row = jnp.where(bit == 0, angles[level, 0], angles[level, 1])
                segment = lax.dynamic_slice_in_dim(row, half * BEAMS, BEAMS, 0)
                total = total + child_term(range_band, sample_window, weights, shifts[level, child], segment)
            return (0.70710678 * total).astype(jnp.bfloat16)

        blocks = lax.map(one_block, jnp.arange(NSUB, dtype=jnp.int32))
        current = jnp.transpose(blocks, (1, 0, 2, 3)).reshape(2, NSUB * BEAMS, R)
    return current
```

```python
import functools

import jax
import jax.numpy as jnp
from jax import lax
from jax.experimental import pallas as pl
from jax.experimental.pallas import tpu as pltpu
from jax.sharding import PartitionSpec as P

MESH = pl.DeviceIdType.MESH
LANES = 128
CHUNK = 256
GAP = 2


def tables(ukern, rkern, angles, taps, half_table, count):
    levels, utaps = half_table.shape[0], ukern.shape[1]
    window = (count + utaps) // 2
    me = lax.axis_index("pulse")
    half = half_table[:, me]
    own_bit = jnp.right_shift(me, jnp.arange(levels, dtype=jnp.int32)) & 1
    by_child = jnp.where((own_bit == 0)[:, None, None], angles, angles[:, ::-1])
    segment = jnp.where(
        (half == 0)[:, None, None], by_child[:, :, :count], by_child[:, :, count:]
    )
    cosine = 0.70710678 * jnp.cos(segment)
    sine = 0.70710678 * jnp.sin(segment)
    turn = jnp.stack([jnp.stack([cosine, -sine], 2), jnp.stack([sine, cosine], 2)], 2)
    phases = jnp.arange(rkern.shape[0], dtype=jnp.int32)
    weights = jnp.sum(
        jnp.where((taps[:, :, None] == phases)[..., None], rkern[None, None], 0.0), axis=2
    )
    beam = jnp.arange(count, dtype=jnp.int32)
    kernel = jnp.where(
        (beam % 2 == 0)[:, None], ukern[0].astype(jnp.float32), ukern[1].astype(jnp.float32)
    )

    def one(child, rows, step):
        first = utaps // 2 - 1 - step * half
        offset = (
            first[:, None, None]
            + jnp.arange(rows, dtype=jnp.int32)[None, None, :]
            - (beam // 2)[None, :, None]
        )
        band = jnp.sum(
            jnp.where(
                offset[..., None] == jnp.arange(utaps, dtype=jnp.int32),
                kernel[None, :, None, :],
                0.0,
            ),
            axis=3,
        )
        matrix = (
            turn[:, child].transpose(0, 1, 3, 2)[:, :, :, None, :, None]
            * weights[:, None, :, :, None, None]
            * band[:, None, :, None, None, :]
        )
        return matrix.reshape(levels, 2 * count, -1).astype(jnp.bfloat16)

    return one(0, count, count // 2), one(1, window, utaps // 2)


def shifted_taps(left, mid, right, shift, ntaps):
    width = mid.shape[1]
    full = jnp.concatenate([left, mid, right], axis=1).astype(jnp.float32)
    total = full.shape[1]
    out = []
    for tap in range(ntaps):
        amount = lax.rem(2 * total - (shift + tap - 1), total)
        moved = pltpu.roll(full, amount, 1)
        out.append(moved[:, LANES : LANES + width].astype(jnp.bfloat16))
    return jnp.concatenate(out, axis=0)


def merge_kernel(
    window, ntaps, shifts_ref, half_ref, x_ref, own_ref, far_ref, out_ref,
    block, outbox, inbox, send_sem, recv_sem,
):
    levels, count = own_ref.shape[0], own_ref.shape[1] // 2
    chunks = inbox.shape[1] - 2
    me = lax.axis_index("pulse")
    partners = []
    for level in range(levels):
        bit = lax.rem(me // 2**level, 2)
        partners.append(me + (1 - 2 * bit) * 2**level)

    barrier = pltpu.get_barrier_semaphore()
    for partner in partners:
        pl.semaphore_signal(barrier, inc=1, device_id={"pulse": partner}, device_id_type=MESH)
    pl.semaphore_wait(barrier, levels)

    for level in range(levels):
        for edge in (0, chunks + 1):
            block[level, edge] = jnp.zeros_like(block[level, edge])
            inbox[level, edge] = jnp.zeros_like(inbox[level, edge])

    def copy(level, chunk):
        return pltpu.make_async_remote_copy(
            src_ref=outbox.at[level, chunk],
            dst_ref=inbox.at[level, chunk + 1],
            send_sem=send_sem.at[level, chunk],
            recv_sem=recv_sem.at[level, chunk],
            device_id={"pulse": partners[level]},
            device_id_type=MESH,
        )

    def hand_over(level, chunk, value):
        block[level, chunk + 1] = value
        high = half_ref[level, me] == 0
        parts = []
        for part in range(2):
            rows = value[part * count : (part + 1) * count]
            parts.append(jnp.where(high, rows[count - window :], rows[:window]))
        outbox[level, chunk] = jnp.concatenate(parts, axis=0)
        copy(level, chunk).start()

    def pieces(ref, level, chunk):
        return (
            ref[level, chunk, :, CHUNK - LANES :],
            ref[level, chunk + 1],
            ref[level, chunk + 2, :, :LANES],
        )

    def work(level, chunk):
        partner = partners[level]
        near = shifted_taps(*pieces(block, level, chunk), shifts_ref[level, me], ntaps)
        far = shifted_taps(*pieces(inbox, level, chunk), shifts_ref[level, partner], ntaps)
        total = jnp.dot(own_ref[level], near, preferred_element_type=jnp.float32)
        total = total + jnp.dot(far_ref[level], far, preferred_element_type=jnp.float32)
        value = total.astype(jnp.bfloat16)
        if level + 1 < levels:
            hand_over(level + 1, chunk, value)
        else:
            out_ref[:, pl.ds(pl.multiple_of(chunk * CHUNK, CHUNK), CHUNK)] = value

    @pl.loop(0, chunks)
    def _(chunk):
        columns = pl.ds(pl.multiple_of(chunk * CHUNK, CHUNK), CHUNK)
        hand_over(0, chunk, x_ref[:, columns])

    last_start = (levels - 1) * GAP

    @pl.loop(0, chunks + 1 + last_start)
    def _(step):
        for level in range(levels):
            coming = step - level * GAP

            @pl.when((coming >= 0) & (coming < chunks))
            def _():
                copy(level, coming).wait_recv()

            @pl.when((coming >= 1) & (coming <= chunks))
            def _():
                work(level, coming - 1)

    for level in range(levels):

        @pl.loop(0, chunks)
        def _(chunk):
            copy(level, chunk).wait_send()


def on_device(beams, ukern, rkern, angles, taps, shifts, half_table):
    parts, count, bins = beams.shape
    levels, utaps, ntaps = half_table.shape[0], ukern.shape[1], rkern.shape[1]
    window = (count + utaps) // 2
    chunks = bins // CHUNK
    own, far = tables(ukern, rkern, angles, taps, half_table, count)
    vmem = pl.BlockSpec(memory_space=pltpu.VMEM)
    smem = pl.BlockSpec(memory_space=pltpu.SMEM)
    merged = pl.pallas_call(
        functools.partial(merge_kernel, window, ntaps),
        out_shape=jax.ShapeDtypeStruct((parts * count, bins), jnp.bfloat16),
        in_specs=[smem, smem, vmem, vmem, vmem],
        out_specs=vmem,
        scratch_shapes=[
            pltpu.VMEM((levels, chunks + 2, parts * count, CHUNK), jnp.bfloat16),
            pltpu.VMEM((levels, chunks, parts * window, CHUNK), jnp.bfloat16),
            pltpu.VMEM((levels, chunks + 2, parts * window, CHUNK), jnp.bfloat16),
            pltpu.SemaphoreType.DMA((levels, chunks)),
            pltpu.SemaphoreType.DMA((levels, chunks)),
        ],
        compiler_params=pltpu.CompilerParams(collective_id=0, has_side_effects=True),
    )(shifts, half_table, beams.reshape(parts * count, bins), own, far)
    return merged.reshape(parts, count, bins)


def solution(mesh):
    in_specs = (
        P(None, ("scene", "pulse"), None),
        P(),
        P(),
        P(),
        P(None, ("scene", "pulse")),
        P(),
        P(),
    )
    out_specs = P(None, ("scene", "pulse"), None)
    return jax.shard_map(
        on_device, mesh=mesh, in_specs=in_specs, out_specs=out_specs, check_vma=False
    )
```

```python
import functools

import jax
import jax.numpy as jnp
from jax import lax
from jax.experimental import pallas as pl
from jax.experimental.pallas import tpu as pltpu
from jax.sharding import PartitionSpec as P

MESH = pl.DeviceIdType.MESH
LANES = 128
CHUNK = 256
ROLLED = jnp.bfloat16
GAP = 2


def band_base(ukern_ref, count):
    utaps = ukern_ref.shape[1]
    beam = lax.broadcasted_iota(jnp.int32, (count, LANES), 0)
    tap = lax.broadcasted_iota(jnp.int32, (count, LANES), 1) - lax.div(beam, 2) - 1
    even = lax.rem(beam, 2) == 0
    base = jnp.zeros((count, LANES), jnp.float32)
    for k in range(utaps):
        base = jnp.where(tap == k, jnp.where(even, ukern_ref[0, k], ukern_ref[1, k]), base)
    return base


def band(base, first, rows):
    lane = lax.broadcasted_iota(jnp.int32, base.shape, 1)
    low = pltpu.roll(base, lax.rem(2 * LANES - first, LANES), 1)
    high = pltpu.roll(base, lax.rem(2 * LANES - first + rows, LANES), 1)
    return jnp.where(lane < rows, low, high)


def level_matrix(base, first, rows, segment, weights):
    cosine = 0.70710678 * jnp.cos(segment)
    sine = 0.70710678 * jnp.sin(segment)
    turns = (jnp.concatenate([cosine, sine], 1), jnp.concatenate([-sine, cosine], 1))
    lines = [jnp.concatenate([w, w], 1) * turn for w in weights for turn in turns]
    columns = jnp.transpose(jnp.concatenate(lines, axis=0))
    one = band(base, first, rows)
    both = jnp.concatenate([one, one], axis=0)
    lane = lax.broadcasted_iota(jnp.int32, both.shape, 1)
    out = []
    for tap in range(len(weights)):
        scale = jnp.where(
            lane < rows, columns[:, 2 * tap : 2 * tap + 1], columns[:, 2 * tap + 1 : 2 * tap + 2]
        )
        out.append((scale * both)[:, : 2 * rows])
    return jnp.concatenate(out, axis=1)


def shifted_taps(tiles, shift, ntaps):
    lane = lax.broadcasted_iota(jnp.int32, tiles[0].shape, 1)
    out = []
    for tap in range(ntaps):
        move = shift + (tap - 1)
        back = move < 0
        place = lax.rem(move + LANES, LANES)
        turned = [
            pltpu.roll(jnp.where(back, low, high), lax.rem(LANES - place, LANES), 1)
            for low, high in zip(tiles[:-1], tiles[1:])
        ]
        keep = lane < LANES - place
        moved = [jnp.where(keep, low, high) for low, high in zip(turned[:-1], turned[1:])]
        out.append(jnp.concatenate(moved, axis=1).astype(jnp.bfloat16))
    return jnp.concatenate(out, axis=0)


def merge_kernel(
    window, shifts_ref, half_ref, rkern_ref, ukern_ref, angles_ref, taps_ref, x_ref, out_ref,
    block, outbox, inbox, own_ref, far_ref, send_sem, recv_sem,
):
    levels, count = own_ref.shape[0], own_ref.shape[1] // 2
    phases, ntaps = rkern_ref.shape
    chunks = inbox.shape[1] - 2
    me = lax.axis_index("pulse")
    partners = []
    for level in range(levels):
        bit = lax.rem(me // 2**level, 2)
        partners.append(me + (1 - 2 * bit) * 2**level)

    barrier = pltpu.get_barrier_semaphore()
    for partner in partners:
        pl.semaphore_signal(barrier, inc=1, device_id={"pulse": partner}, device_id_type=MESH)
    pl.semaphore_wait(barrier, levels)

    for level in range(levels):
        for edge in (0, chunks + 1):
            block[level, edge] = jnp.zeros_like(block[level, edge])
            inbox[level, edge] = jnp.zeros_like(inbox[level, edge])

    def copy(level, chunk):
        return pltpu.make_async_remote_copy(
            src_ref=outbox.at[level, chunk],
            dst_ref=inbox.at[level, chunk + 1],
            send_sem=send_sem.at[level, chunk],
            recv_sem=recv_sem.at[level, chunk],
            device_id={"pulse": partners[level]},
            device_id_type=MESH,
        )

    def hand_over(level, chunk, value):
        block[level, chunk + 1] = value
        high = half_ref[level, me] == 0
        parts = []
        for part in range(2):
            rows = value[part * count : (part + 1) * count]
            parts.append(jnp.where(high, rows[count - window :], rows[:window]))
        outbox[level, chunk] = jnp.concatenate(parts, axis=0)
        copy(level, chunk).start()

    def pieces(ref, level, chunk):
        parts = [ref[level, chunk, :, CHUNK - LANES :]]
        for start in range(0, CHUNK, LANES):
            parts.append(ref[level, chunk + 1, :, start : start + LANES])
        parts.append(ref[level, chunk + 2, :, :LANES])
        return [part.astype(ROLLED) for part in parts]

    def work(level, chunk):
        partner = partners[level]
        near = shifted_taps(pieces(block, level, chunk), shifts_ref[level, me], ntaps)
        far = shifted_taps(pieces(inbox, level, chunk), shifts_ref[level, partner], ntaps)
        total = jnp.dot(own_ref[level], near, preferred_element_type=jnp.float32)
        total = total + jnp.dot(far_ref[level], far, preferred_element_type=jnp.float32)
        value = total.astype(jnp.bfloat16)
        if level + 1 < levels:
            hand_over(level + 1, chunk, value)
        else:
            out_ref[:, pl.ds(pl.multiple_of(chunk * CHUNK, CHUNK), CHUNK)] = value

    @pl.loop(0, chunks)
    def _(chunk):
        columns = pl.ds(pl.multiple_of(chunk * CHUNK, CHUNK), CHUNK)
        hand_over(0, chunk, x_ref[:, columns])

    base = band_base(ukern_ref, count)
    for level in range(levels):
        high = half_ref[level, me]
        segments = jnp.where(high == 0, angles_ref[level, :, :count], angles_ref[level, :, count:])
        upper = lax.rem(me // 2**level, 2) == 1
        here = jnp.where(upper, segments[1:2], segments[0:1])
        there = jnp.where(upper, segments[0:1], segments[1:2])
        phase = taps_ref[level : level + 1]
        weights = [jnp.zeros(phase.shape, jnp.float32)] * ntaps
        for number in range(phases):
            hit = phase == number
            weights = [jnp.where(hit, rkern_ref[number, t], w) for t, w in enumerate(weights)]
        pad = window - count // 2
        first = pad - high * (count // 2)
        own = level_matrix(base, first, count, here, weights)
        own_ref[level] = own.astype(jnp.bfloat16)
        far = level_matrix(base, first + high * (count - window), window, there, weights)
        far_ref[level] = far.astype(jnp.bfloat16)

    last_start = (levels - 1) * GAP

    @pl.loop(0, chunks + 1 + last_start)
    def _(step):
        for level in range(levels):
            coming = step - level * GAP

            @pl.when((coming >= 0) & (coming < chunks))
            def _():
                copy(level, coming).wait_recv()

            @pl.when((coming >= 1) & (coming <= chunks))
            def _():
                work(level, coming - 1)

    for level in range(levels):

        @pl.loop(0, chunks)
        def _(chunk):
            copy(level, chunk).wait_send()


def on_device(beams, ukern, rkern, angles, taps, shifts, half_table):
    parts, count, bins = beams.shape
    levels, utaps, ntaps = half_table.shape[0], ukern.shape[1], rkern.shape[1]
    window = (count + utaps) // 2
    chunks = bins // CHUNK
    vmem = pl.BlockSpec(memory_space=pltpu.VMEM)
    smem = pl.BlockSpec(memory_space=pltpu.SMEM)
    merged = pl.pallas_call(
        functools.partial(merge_kernel, window),
        out_shape=jax.ShapeDtypeStruct((parts * count, bins), jnp.bfloat16),
        in_specs=[smem, smem, smem, smem, vmem, vmem, vmem],
        out_specs=vmem,
        scratch_shapes=[
            pltpu.VMEM((levels, chunks + 2, parts * count, CHUNK), jnp.bfloat16),
            pltpu.VMEM((levels, chunks, parts * window, CHUNK), jnp.bfloat16),
            pltpu.VMEM((levels, chunks + 2, parts * window, CHUNK), jnp.bfloat16),
            pltpu.VMEM((levels, parts * count, ntaps * parts * count), jnp.bfloat16),
            pltpu.VMEM((levels, parts * count, ntaps * parts * window), jnp.bfloat16),
            pltpu.SemaphoreType.DMA((levels, chunks)),
            pltpu.SemaphoreType.DMA((levels, chunks)),
        ],
        compiler_params=pltpu.CompilerParams(collective_id=0, has_side_effects=True),
    )(
        shifts,
        half_table,
        rkern,
        ukern.astype(jnp.float32),
        angles,
        taps,
        beams.reshape(parts * count, bins),
    )
    return merged.reshape(parts, count, bins)


def solution(mesh):
    in_specs = (
        P(None, ("scene", "pulse"), None),
        P(),
        P(),
        P(),
        P(None, ("scene", "pulse")),
        P(),
        P(),
    )
    out_specs = P(None, ("scene", "pulse"), None)
    return jax.shard_map(
        on_device, mesh=mesh, in_specs=in_specs, out_specs=out_specs, check_vma=False
    )
```

```python
import functools

import jax
import jax.numpy as jnp
from jax import lax
from jax.experimental import pallas as pl
from jax.experimental.pallas import tpu as pltpu
from jax.sharding import PartitionSpec as P

MESH = pl.DeviceIdType.MESH
LANES = 128
CHUNK = 256
ROLLED = jnp.bfloat16
GAP = 3
LAST = 4


def band_base(ukern, count):
    utaps = ukern.shape[1]
    beam = lax.broadcasted_iota(jnp.int32, (count, LANES), 0)
    tap = lax.broadcasted_iota(jnp.int32, (count, LANES), 1) - lax.div(beam, 2) - 1
    even = lax.rem(beam, 2) == 0
    base = jnp.zeros((count, LANES), jnp.float32)
    for k in range(utaps):
        column = ukern[:, k : k + 1]
        base = jnp.where(tap == k, jnp.where(even, column[0:1], column[1:2]), base)
    return base


def band(base, first, rows):
    lane = lax.broadcasted_iota(jnp.int32, base.shape, 1)
    low = pltpu.roll(base, lax.rem(2 * LANES - first, LANES), 1)
    high = pltpu.roll(base, lax.rem(2 * LANES - first + rows, LANES), 1)
    return jnp.where(lane < rows, low, high)


def level_matrix(base, first, rows, segment, weights):
    cosine = 0.70710678 * jnp.cos(segment)
    sine = 0.70710678 * jnp.sin(segment)
    turns = (jnp.concatenate([cosine, sine], 1), jnp.concatenate([-sine, cosine], 1))
    lines = [jnp.concatenate([w, w], 1) * turn for w in weights for turn in turns]
    columns = jnp.transpose(jnp.concatenate(lines, axis=0))
    one = band(base, first, rows)
    both = jnp.concatenate([one, one], axis=0)
    lane = lax.broadcasted_iota(jnp.int32, both.shape, 1)
    out = []
    for tap in range(len(weights)):
        scale = jnp.where(
            lane < rows, columns[:, 2 * tap : 2 * tap + 1], columns[:, 2 * tap + 1 : 2 * tap + 2]
        )
        out.append((scale * both)[:, : 2 * rows])
    return jnp.concatenate(out, axis=1)


def two_terms(matrix):
    high = matrix.astype(jnp.bfloat16)
    rest = (matrix - high.astype(jnp.float32)).astype(jnp.bfloat16)
    return jnp.concatenate([high, rest], axis=0)


def shifted_taps(tiles, shift, ntaps):
    lane = lax.broadcasted_iota(jnp.int32, tiles[0].shape, 1)
    out = []
    for tap in range(ntaps):
        move = shift + (tap - 1)
        back = move < 0
        place = lax.rem(move + LANES, LANES)
        turned = [
            pltpu.roll(jnp.where(back, low, high), lax.rem(LANES - place, LANES), 1)
            for low, high in zip(tiles[:-1], tiles[1:])
        ]
        keep = lane < LANES - place
        moved = [jnp.where(keep, low, high) for low, high in zip(turned[:-1], turned[1:])]
        out.append(jnp.concatenate(moved, axis=1).astype(jnp.bfloat16))
    return jnp.concatenate(out, axis=0)


def merge_kernel(
    window, shifts_ref, half_ref, rkern_ref, ukern_ref, angles_ref, taps_ref, x_ref, out_ref,
    block, outbox, inbox, own_ref, far_ref, result, send_sem, recv_sem, out_sem,
):
    levels, count = own_ref.shape[0], own_ref.shape[1] // 4
    ntaps, phases = rkern_ref.shape
    chunks = inbox.shape[1] - 2
    me = lax.axis_index("pulse")
    partners = []
    for level in range(levels):
        bit = lax.rem(me // 2**level, 2)
        partners.append(me + (1 - 2 * bit) * 2**level)

    barrier = pltpu.get_barrier_semaphore()
    for partner in partners:
        pl.semaphore_signal(barrier, inc=1, device_id={"pulse": partner}, device_id_type=MESH)
    pl.semaphore_wait(barrier, levels)

    for level in range(levels):
        for edge in (0, chunks + 1):
            block[level, edge] = jnp.zeros_like(block[level, edge])
            inbox[level, edge] = jnp.zeros_like(inbox[level, edge])

    def copy(level, chunk):
        return pltpu.make_async_remote_copy(
            src_ref=outbox.at[level, chunk],
            dst_ref=inbox.at[level, chunk + 1],
            send_sem=send_sem.at[level, chunk],
            recv_sem=recv_sem.at[level, chunk],
            device_id={"pulse": partners[level]},
            device_id_type=MESH,
        )

    def put_out(chunk):
        columns = pl.ds(pl.multiple_of(chunk * CHUNK, CHUNK), CHUNK)
        return pltpu.make_async_copy(result.at[chunk], out_ref.at[:, columns], out_sem.at[chunk])

    def hand_over(level, chunk, value):
        block[level, chunk + 1] = value
        high = half_ref[level, me] == 0
        parts = []
        for part in range(2):
            rows = value[part * count : (part + 1) * count]
            parts.append(jnp.where(high, rows[count - window :], rows[:window]))
        outbox[level, chunk] = jnp.concatenate(parts, axis=0)
        copy(level, chunk).start()

    def pieces(ref, level, chunk):
        parts = [ref[level, chunk, :, CHUNK - LANES :]]
        for start in range(0, CHUNK, LANES):
            parts.append(ref[level, chunk + 1, :, start : start + LANES])
        parts.append(ref[level, chunk + 2, :, :LANES])
        return [part.astype(ROLLED) for part in parts]

    def work(level, chunk):
        partner = partners[level]
        near = shifted_taps(pieces(block, level, chunk), shifts_ref[level, me], ntaps)
        far = shifted_taps(pieces(inbox, level, chunk), shifts_ref[level, partner], ntaps)
        total = jnp.dot(own_ref[level], near, preferred_element_type=jnp.float32)
        total = total + jnp.dot(far_ref[level], far, preferred_element_type=jnp.float32)
        total = total[: 2 * count] + total[2 * count :]
        if level + 1 < levels:
            hand_over(level + 1, chunk, total.astype(jnp.bfloat16))
        else:
            result[chunk] = total
            put_out(chunk).start()

    @pl.loop(0, chunks)
    def _(chunk):
        columns = pl.ds(pl.multiple_of(chunk * CHUNK, CHUNK), CHUNK)
        hand_over(0, chunk, x_ref[:, columns])

    base = band_base(ukern_ref[...].astype(jnp.float32), count)
    rkern = rkern_ref[...]
    for level in range(levels):
        high = half_ref[level, me]
        segments = jnp.where(high == 0, angles_ref[level, :, :count], angles_ref[level, :, count:])
        upper = lax.rem(me // 2**level, 2) == 1
        here = jnp.where(upper, segments[1:2], segments[0:1])
        there = jnp.where(upper, segments[0:1], segments[1:2])
        phase = taps_ref[level : level + 1]
        weights = [jnp.zeros(phase.shape, jnp.float32)] * ntaps
        for number in range(phases):
            hit = phase == number
            weights = [jnp.where(hit, rkern[t : t + 1, number : number + 1], w)
                for t, w in enumerate(weights)
           ]
        pad = window - count // 2
        first = pad - high * (count // 2)
        own = level_matrix(base, first, count, here, weights)
        own_ref[level] = two_terms(own)
        far = level_matrix(base, first + high * (count - window), window, there, weights)
        far_ref[level] = two_terms(far)

    starts = [level * GAP for level in range(levels)]
    starts[-1] += LAST

    @pl.loop(0, chunks + 1 + starts[-1])
    def _(step):
        for level in range(levels):
            coming = step - starts[level]

            @pl.when((coming >= 0) & (coming < chunks))
            def _():
                copy(level, coming).wait_recv()

            @pl.when((coming >= 1) & (coming <= chunks))
            def _():
                work(level, coming - 1)

    for level in range(levels):

        @pl.loop(0, chunks)
        def _(chunk):
            copy(level, chunk).wait_send()

    @pl.loop(0, chunks)
    def _(chunk):
        put_out(chunk).wait()


def on_device(beams, ukern, rkern, angles, taps, shifts, half_table):
    parts, count, bins = beams.shape
    levels, utaps, ntaps = half_table.shape[0], ukern.shape[1], rkern.shape[1]
    window = (count + utaps) // 2
    chunks = bins // CHUNK
    vmem = pl.BlockSpec(memory_space=pltpu.VMEM)
    smem = pl.BlockSpec(memory_space=pltpu.SMEM)
    merged = pl.pallas_call(
        functools.partial(merge_kernel, window),
        out_shape=jax.ShapeDtypeStruct((parts * count, bins), jnp.float32),
        in_specs=[smem, smem, vmem, vmem, vmem, vmem, vmem],
        out_specs=pl.BlockSpec(memory_space=pl.ANY),
        scratch_shapes=[
            pltpu.VMEM((levels, chunks + 2, parts * count, CHUNK), jnp.bfloat16),
            pltpu.VMEM((levels, chunks, parts * window, CHUNK), jnp.bfloat16),
            pltpu.VMEM((levels, chunks + 2, parts * window, CHUNK), jnp.bfloat16),
            pltpu.VMEM((levels, 2 * parts * count, ntaps * parts * count), jnp.bfloat16),
            pltpu.VMEM((levels, 2 * parts * count, ntaps * parts * window), jnp.bfloat16),
            pltpu.VMEM((chunks, parts * count, CHUNK), jnp.float32),
            pltpu.SemaphoreType.DMA((levels, chunks)),
            pltpu.SemaphoreType.DMA((levels, chunks)),
            pltpu.SemaphoreType.DMA((chunks,)),
        ],
        compiler_params=pltpu.CompilerParams(collective_id=0, has_side_effects=True),
    )(
        shifts,
        half_table,
        rkern.T,
        ukern,
        angles,
        taps,
        beams.reshape(parts * count, bins),
    )
    return merged.astype(jnp.bfloat16).reshape(parts, count, bins)


def solution(mesh):
    in_specs = (
        P(None, ("scene", "pulse"), None),
        P(),
        P(),
        P(),
        P(None, ("scene", "pulse")),
        P(),
        P(),
    )
    out_specs = P(None, ("scene", "pulse"), None)
    return jax.shard_map(
        on_device, mesh=mesh, in_specs=in_specs, out_specs=out_specs, check_vma=False
    )
```

```python
import functools

import jax
import jax.numpy as jnp
from jax import lax
from jax.experimental import pallas as pl
from jax.experimental.pallas import tpu as pltpu
from jax.sharding import PartitionSpec as P

MESH = pl.DeviceIdType.MESH
LANES = 128
CHUNK = 256
ROLLED = jnp.bfloat16
FIRST = 3
GAP = 3
LAST = 4


def band_base(ukern, count):
    utaps = ukern.shape[1]
    beam = lax.broadcasted_iota(jnp.int32, (count, LANES), 0)
    tap = lax.broadcasted_iota(jnp.int32, (count, LANES), 1) - lax.div(beam, 2) - 1
    even = lax.rem(beam, 2) == 0
    base = jnp.zeros((count, LANES), jnp.float32)
    for k in range(utaps):
        column = ukern[:, k : k + 1]
        base = jnp.where(tap == k, jnp.where(even, column[0:1], column[1:2]), base)
    return base


def band(base, first, rows):
    lane = lax.broadcasted_iota(jnp.int32, base.shape, 1)
    low = pltpu.roll(base, lax.rem(2 * LANES - first, LANES), 1)
    high = pltpu.roll(base, lax.rem(2 * LANES - first + rows, LANES), 1)
    return jnp.where(lane < rows, low, high)


def level_matrix(base, first, rows, segment, weights):
    cosine = 0.70710678 * jnp.cos(segment)
    sine = 0.70710678 * jnp.sin(segment)
    turns = (jnp.concatenate([cosine, sine], 1), jnp.concatenate([-sine, cosine], 1))
    lines = [jnp.concatenate([w, w], 1) * turn for w in weights for turn in turns]
    columns = jnp.transpose(jnp.concatenate(lines, axis=0))
    one = band(base, first, rows)
    both = jnp.concatenate([one, one], axis=0)
    lane = lax.broadcasted_iota(jnp.int32, both.shape, 1)
    out = []
    for tap in range(len(weights)):
        scale = jnp.where(
            lane < rows, columns[:, 2 * tap : 2 * tap + 1], columns[:, 2 * tap + 1 : 2 * tap + 2]
        )
        out.append((scale * both)[:, : 2 * rows])
    return jnp.concatenate(out, axis=1)


def two_terms(matrix):
    high = matrix.astype(jnp.bfloat16)
    rest = (matrix - high.astype(jnp.float32)).astype(jnp.bfloat16)
    return jnp.concatenate([high, rest], axis=0)


def shifted_taps(tiles, shift, ntaps):
    lane = lax.broadcasted_iota(jnp.int32, tiles[0].shape, 1)
    out = []
    for tap in range(ntaps):
        move = shift + (tap - 1)
        back = move < 0
        place = lax.rem(move + LANES, LANES)
        turned = [
            pltpu.roll(jnp.where(back, low, high), lax.rem(LANES - place, LANES), 1)
            for low, high in zip(tiles[:-1], tiles[1:])
        ]
        keep = lane < LANES - place
        moved = [jnp.where(keep, low, high) for low, high in zip(turned[:-1], turned[1:])]
        out.append(jnp.concatenate(moved, axis=1).astype(jnp.bfloat16))
    return jnp.concatenate(out, axis=0)


def merge_kernel(
    window, shifts_ref, half_ref, rkern_ref, ukern_ref, angles_ref, taps_ref, x_ref, out_ref,
    block, outbox, inbox, own_ref, far_ref, result, send_sem, recv_sem, out_sem,
):
    levels, count = own_ref.shape[0], own_ref.shape[1] // 4
    ntaps, phases = rkern_ref.shape
    chunks = inbox.shape[1] - 2
    me = lax.axis_index("pulse")
    partners = []
    for level in range(levels):
        bit = lax.rem(me // 2**level, 2)
        partners.append(me + (1 - 2 * bit) * 2**level)

    barrier = pltpu.get_barrier_semaphore()
    for partner in partners:
        pl.semaphore_signal(barrier, inc=1, device_id={"pulse": partner}, device_id_type=MESH)
    pl.semaphore_wait(barrier, levels)

    for level in range(levels):
        for edge in (0, chunks + 1):
            block[level, edge] = jnp.zeros_like(block[level, edge])
            inbox[level, edge] = jnp.zeros_like(inbox[level, edge])

    def copy(level, chunk):
        return pltpu.make_async_remote_copy(
            src_ref=outbox.at[level, chunk],
            dst_ref=inbox.at[level, chunk + 1],
            send_sem=send_sem.at[level, chunk],
            recv_sem=recv_sem.at[level, chunk],
            device_id={"pulse": partners[level]},
            device_id_type=MESH,
        )

    def put_out(chunk):
        columns = pl.ds(pl.multiple_of(chunk * CHUNK, CHUNK), CHUNK)
        return pltpu.make_async_copy(result.at[chunk], out_ref.at[:, columns], out_sem.at[chunk])

    def hand_over(level, chunk, value):
        block[level, chunk + 1] = value
        high = half_ref[level, me] == 0
        parts = []
        for part in range(2):
            rows = value[part * count : (part + 1) * count]
            parts.append(jnp.where(high, rows[count - window :], rows[:window]))
        outbox[level, chunk] = jnp.concatenate(parts, axis=0)
        copy(level, chunk).start()

    def pieces(ref, level, chunk):
        parts = [ref[level, chunk, :, CHUNK - LANES :]]
        for start in range(0, CHUNK, LANES):
            parts.append(ref[level, chunk + 1, :, start : start + LANES])
        parts.append(ref[level, chunk + 2, :, :LANES])
        return [part.astype(ROLLED) for part in parts]

    def work(level, chunk):
        partner = partners[level]
        near = shifted_taps(pieces(block, level, chunk), shifts_ref[level, me], ntaps)
        far = shifted_taps(pieces(inbox, level, chunk), shifts_ref[level, partner], ntaps)
        total = jnp.dot(own_ref[level], near, preferred_element_type=jnp.float32)
        total = total + jnp.dot(far_ref[level], far, preferred_element_type=jnp.float32)
        total = total[: 2 * count] + total[2 * count :]
        if level + 1 < levels:
            hand_over(level + 1, chunk, total.astype(jnp.bfloat16))
        else:
            result[chunk] = total.astype(jnp.bfloat16)
            put_out(chunk).start()

    @pl.loop(0, chunks)
    def _(chunk):
        columns = pl.ds(pl.multiple_of(chunk * CHUNK, CHUNK), CHUNK)
        hand_over(0, chunk, x_ref[:, columns])

    base = band_base(ukern_ref[...].astype(jnp.float32), count)
    rkern = rkern_ref[...]
    def build(level):
        high = half_ref[level, me]
        segments = jnp.where(high == 0, angles_ref[level, :, :count], angles_ref[level, :, count:])
        upper = lax.rem(me // 2**level, 2) == 1
        here = jnp.where(upper, segments[1:2], segments[0:1])
        there = jnp.where(upper, segments[0:1], segments[1:2])
        phase = taps_ref[level : level + 1]
        weights = [jnp.zeros(phase.shape, jnp.float32)] * ntaps
        for number in range(phases):
            hit = phase == number
            weights = [jnp.where(hit, rkern[t : t + 1, number : number + 1], w)
                for t, w in enumerate(weights)
           ]
        pad = window - count // 2
        first = pad - high * (count // 2)
        own = level_matrix(base, first, count, here, weights)
        own_ref[level] = two_terms(own)
        far = level_matrix(base, first + high * (count - window), window, there, weights)
        far_ref[level] = two_terms(far)

    starts = [0] + [FIRST + level * GAP for level in range(levels - 1)]
    starts[-1] += LAST

    @pl.loop(0, chunks + 1 + starts[-1])
    def _(step):
        for level in range(levels):
            coming = step - starts[level]

            @pl.when(coming == 0)
            def _():
                build(level)

            @pl.when((coming >= 0) & (coming < chunks))
            def _():
                copy(level, coming).wait_recv()

            @pl.when((coming >= 1) & (coming <= chunks))
            def _():
                work(level, coming - 1)

    for level in range(levels):

        @pl.loop(0, chunks)
        def _(chunk):
            copy(level, chunk).wait_send()

    @pl.loop(0, chunks)
    def _(chunk):
        put_out(chunk).wait()


def on_device(beams, ukern, rkern, angles, taps, shifts, half_table):
    parts, count, bins = beams.shape
    levels, utaps, ntaps = half_table.shape[0], ukern.shape[1], rkern.shape[1]
    window = (count + utaps) // 2
    chunks = bins // CHUNK
    vmem = pl.BlockSpec(memory_space=pltpu.VMEM)
    smem = pl.BlockSpec(memory_space=pltpu.SMEM)
    merged = pl.pallas_call(
        functools.partial(merge_kernel, window),
        out_shape=jax.ShapeDtypeStruct((parts * count, bins), jnp.bfloat16),
        in_specs=[smem, smem, vmem, vmem, vmem, vmem, vmem],
        out_specs=pl.BlockSpec(memory_space=pl.ANY),
        scratch_shapes=[
            pltpu.VMEM((levels, chunks + 2, parts * count, CHUNK), jnp.bfloat16),
            pltpu.VMEM((levels, chunks, parts * window, CHUNK), jnp.bfloat16),
            pltpu.VMEM((levels, chunks + 2, parts * window, CHUNK), jnp.bfloat16),
            pltpu.VMEM((levels, 2 * parts * count, ntaps * parts * count), jnp.bfloat16),
            pltpu.VMEM((levels, 2 * parts * count, ntaps * parts * window), jnp.bfloat16),
            pltpu.VMEM((chunks, parts * count, CHUNK), jnp.bfloat16),
            pltpu.SemaphoreType.DMA((levels, chunks)),
            pltpu.SemaphoreType.DMA((levels, chunks)),
            pltpu.SemaphoreType.DMA((chunks,)),
        ],
        compiler_params=pltpu.CompilerParams(collective_id=0, has_side_effects=True),
    )(
        shifts,
        half_table,
        rkern.T,
        ukern,
        angles,
        taps,
        beams.reshape(parts * count, bins),
    )
    return merged.reshape(parts, count, bins)


def solution(mesh):
    in_specs = (
        P(None, ("scene", "pulse"), None),
        P(),
        P(),
        P(),
        P(None, ("scene", "pulse")),
        P(),
        P(),
    )
    out_specs = P(None, ("scene", "pulse"), None)
    return jax.shard_map(
        on_device, mesh=mesh, in_specs=in_specs, out_specs=out_specs, check_vma=False
    )
```

```python
import functools

import jax
import jax.numpy as jnp
from jax import lax
from jax.experimental import pallas as pl
from jax.experimental.pallas import tpu as pltpu
from jax.sharding import PartitionSpec as P

MESH = pl.DeviceIdType.MESH
LANES = 128
CHUNK = 256
ROLLED = jnp.bfloat16
FIRST = 4
GAP = 3
LAST = 6


def band_base(ukern, count):
    utaps = ukern.shape[1]
    beam = lax.broadcasted_iota(jnp.int32, (count, LANES), 0)
    tap = lax.broadcasted_iota(jnp.int32, (count, LANES), 1) - lax.div(beam, 2) - 1
    even = lax.rem(beam, 2) == 0
    base = jnp.zeros((count, LANES), jnp.float32)
    for k in range(utaps):
        column = ukern[:, k : k + 1]
        base = jnp.where(tap == k, jnp.where(even, column[0:1], column[1:2]), base)
    return base


def band(base, first, rows):
    lane = lax.broadcasted_iota(jnp.int32, base.shape, 1)
    low = pltpu.roll(base, lax.rem(2 * LANES - first, LANES), 1)
    high = pltpu.roll(base, lax.rem(2 * LANES - first + rows, LANES), 1)
    return jnp.where(lane < rows, low, high)


def level_matrix(base, first, rows, segment, weights):
    cosine = 0.70710678 * jnp.cos(segment)
    sine = 0.70710678 * jnp.sin(segment)
    turns = (jnp.concatenate([cosine, sine], 1), jnp.concatenate([-sine, cosine], 1))
    lines = [jnp.concatenate([w, w], 1) * turn for w in weights for turn in turns]
    columns = jnp.transpose(jnp.concatenate(lines, axis=0))
    one = band(base, first, rows)
    both = jnp.concatenate([one, one], axis=0)
    lane = lax.broadcasted_iota(jnp.int32, both.shape, 1)
    out = []
    for tap in range(len(weights)):
        scale = jnp.where(
            lane < rows, columns[:, 2 * tap : 2 * tap + 1], columns[:, 2 * tap + 1 : 2 * tap + 2]
        )
        out.append((scale * both)[:, : 2 * rows])
    return jnp.concatenate(out, axis=1)


def two_terms(matrix):
    high = matrix.astype(jnp.bfloat16)
    rest = (matrix - high.astype(jnp.float32)).astype(jnp.bfloat16)
    return jnp.concatenate([high, rest], axis=0)


def shifted_taps(tiles, shift, ntaps):
    lane = lax.broadcasted_iota(jnp.int32, tiles[0].shape, 1)
    out = []
    for tap in range(ntaps):
        move = shift + (tap - 1)
        back = move < 0
        place = lax.rem(move + LANES, LANES)
        turned = [
            pltpu.roll(jnp.where(back, low, high), lax.rem(LANES - place, LANES), 1)
            for low, high in zip(tiles[:-1], tiles[1:])
        ]
        keep = lane < LANES - place
        moved = [jnp.where(keep, low, high) for low, high in zip(turned[:-1], turned[1:])]
        out.append(jnp.concatenate(moved, axis=1).astype(jnp.bfloat16))
    return jnp.concatenate(out, axis=0)


def merge_kernel(
    window, shifts_ref, half_ref, rkern_ref, ukern_ref, angles_ref, taps_ref, x_ref, out_ref,
    block, outbox, inbox, own_ref, far_ref, result, send_sem, recv_sem, out_sem,
):
    levels, count = own_ref.shape[0], own_ref.shape[1] // 4
    ntaps, phases = rkern_ref.shape
    chunks = inbox.shape[1] - 2
    me = lax.axis_index("pulse")
    partners = []
    for level in range(levels):
        bit = lax.rem(me // 2**level, 2)
        partners.append(me + (1 - 2 * bit) * 2**level)

    barrier = pltpu.get_barrier_semaphore()
    for partner in partners:
        pl.semaphore_signal(barrier, inc=1, device_id={"pulse": partner}, device_id_type=MESH)
    pl.semaphore_wait(barrier, levels)

    for level in range(levels):
        for edge in (0, chunks + 1):
            block[level, edge] = jnp.zeros_like(block[level, edge])
            inbox[level, edge] = jnp.zeros_like(inbox[level, edge])

    def copy(level, chunk):
        return pltpu.make_async_remote_copy(
            src_ref=outbox.at[level, chunk],
            dst_ref=inbox.at[level, chunk + 1],
            send_sem=send_sem.at[level, chunk],
            recv_sem=recv_sem.at[level, chunk],
            device_id={"pulse": partners[level]},
            device_id_type=MESH,
        )

    def put_out(chunk):
        columns = pl.ds(pl.multiple_of(chunk * CHUNK, CHUNK), CHUNK)
        return pltpu.make_async_copy(result.at[chunk], out_ref.at[:, columns], out_sem.at[chunk])

    def hand_over(level, chunk, value):
        block[level, chunk + 1] = value
        high = half_ref[level, me] == 0
        parts = []
        for part in range(2):
            rows = value[part * count : (part + 1) * count]
            parts.append(jnp.where(high, rows[count - window :], rows[:window]))
        outbox[level, chunk] = jnp.concatenate(parts, axis=0)
        copy(level, chunk).start()

    def pieces(ref, level, chunk):
        parts = [ref[level, chunk, :, CHUNK - LANES :]]
        for start in range(0, CHUNK, LANES):
            parts.append(ref[level, chunk + 1, :, start : start + LANES])
        parts.append(ref[level, chunk + 2, :, :LANES])
        return [part.astype(ROLLED) for part in parts]

    def work(level, chunk):
        partner = partners[level]
        near = shifted_taps(pieces(block, level, chunk), shifts_ref[level, me], ntaps)
        far = shifted_taps(pieces(inbox, level, chunk), shifts_ref[level, partner], ntaps)
        total = jnp.dot(own_ref[level], near, preferred_element_type=jnp.float32)
        total = total + jnp.dot(far_ref[level], far, preferred_element_type=jnp.float32)
        total = total[: 2 * count] + total[2 * count :]
        if level + 1 < levels:
            hand_over(level + 1, chunk, total.astype(jnp.bfloat16))
        else:
            result[chunk] = total.astype(jnp.bfloat16)
            put_out(chunk).start()

    @pl.loop(0, chunks)
    def _(chunk):
        columns = pl.ds(pl.multiple_of(chunk * CHUNK, CHUNK), CHUNK)
        hand_over(0, chunk, x_ref[:, columns])

    base = band_base(ukern_ref[...].astype(jnp.float32), count)
    rkern = rkern_ref[...]
    def build(level):
        high = half_ref[level, me]
        segments = jnp.where(high == 0, angles_ref[level, :, :count], angles_ref[level, :, count:])
        upper = lax.rem(me // 2**level, 2) == 1
        here = jnp.where(upper, segments[1:2], segments[0:1])
        there = jnp.where(upper, segments[0:1], segments[1:2])
        phase = taps_ref[level : level + 1]
        weights = [jnp.zeros(phase.shape, jnp.float32)] * ntaps
        for number in range(phases):
            hit = phase == number
            weights = [jnp.where(hit, rkern[t : t + 1, number : number + 1], w)
                for t, w in enumerate(weights)
           ]
        pad = window - count // 2
        first = pad - high * (count // 2)
        own = level_matrix(base, first, count, here, weights)
        own_ref[level] = two_terms(own)
        far = level_matrix(base, first + high * (count - window), window, there, weights)
        far_ref[level] = two_terms(far)

    starts = [0] + [FIRST + level * GAP for level in range(levels - 1)]
    starts[-1] += LAST

    @pl.loop(0, chunks + 1 + starts[-1])
    def _(step):
        for level in range(levels):
            coming = step - starts[level]

            @pl.when(coming == 0)
            def _():
                build(level)

            @pl.when((coming >= 0) & (coming < chunks))
            def _():
                copy(level, coming).wait_recv()

            @pl.when((coming >= 1) & (coming <= chunks))
            def _():
                work(level, coming - 1)

    for level in range(levels):

        @pl.loop(0, chunks)
        def _(chunk):
            copy(level, chunk).wait_send()

    @pl.loop(0, chunks)
    def _(chunk):
        put_out(chunk).wait()


def on_device(beams, ukern, rkern, angles, taps, shifts, half_table):
    parts, count, bins = beams.shape
    levels, utaps, ntaps = half_table.shape[0], ukern.shape[1], rkern.shape[1]
    window = (count + utaps) // 2
    chunks = bins // CHUNK
    vmem = pl.BlockSpec(memory_space=pltpu.VMEM)
    smem = pl.BlockSpec(memory_space=pltpu.SMEM)
    merged = pl.pallas_call(
        functools.partial(merge_kernel, window),
        out_shape=jax.ShapeDtypeStruct((parts * count, bins), jnp.bfloat16),
        in_specs=[smem, smem, vmem, vmem, vmem, vmem, vmem],
        out_specs=pl.BlockSpec(memory_space=pl.ANY),
        scratch_shapes=[
            pltpu.VMEM((levels, chunks + 2, parts * count, CHUNK), jnp.bfloat16),
            pltpu.VMEM((levels, chunks, parts * window, CHUNK), jnp.bfloat16),
            pltpu.VMEM((levels, chunks + 2, parts * window, CHUNK), jnp.bfloat16),
            pltpu.VMEM((levels, 2 * parts * count, ntaps * parts * count), jnp.bfloat16),
            pltpu.VMEM((levels, 2 * parts * count, ntaps * parts * window), jnp.bfloat16),
            pltpu.VMEM((chunks, parts * count, CHUNK), jnp.bfloat16),
            pltpu.SemaphoreType.DMA((levels, chunks)),
            pltpu.SemaphoreType.DMA((levels, chunks)),
            pltpu.SemaphoreType.DMA((chunks,)),
        ],
        compiler_params=pltpu.CompilerParams(collective_id=0, has_side_effects=True),
    )(
        shifts,
        half_table,
        rkern.T,
        ukern,
        angles,
        taps,
        beams.reshape(parts * count, bins),
    )
    return merged.reshape(parts, count, bins)


def solution(mesh):
    in_specs = (
        P(None, ("scene", "pulse"), None),
        P(),
        P(),
        P(),
        P(None, ("scene", "pulse")),
        P(),
        P(),
    )
    out_specs = P(None, ("scene", "pulse"), None)
    return jax.shard_map(
        on_device, mesh=mesh, in_specs=in_specs, out_specs=out_specs, check_vma=False
    )
```
